32 devices in a mesh: prow: 8 (over y, x, core), pcol: 4 (over z).
Axes of the slice: x: 2, y: 2, z: 4, core: 2. Of those that a mesh axis runs over, the one named last changes fastest.
Arguments:
- inverse_trailing: bfloat16 [18432, 18432], P('prow', 'pcol'), may hold values from -6 to 6
- panel: bfloat16 [18432, 256], P('prow'), may hold values from -0.0625 to 0.0625
- supernode_inverse: float32 [256, 256], replicated, may hold values from -6 to 6
- block_live: int32 [72], replicated, may hold values from 0 to 1, as said below
Outputs:
- column_inverse: float32 [18432, 256], P('prow')
- diagonal_inverse: float32 [256, 256], replicated
The draws below stay inside these ranges and needn't reach their ends.
Inputs may be any that keep to these rules, and one draw needn't show every extreme that they name: Each aligned group of 9 consecutive block rows (the rows of one index of prow) holds at least one block row with block_live 1.
All inputs are finite; a program needn't handle non-finite values.
Results may differ from the reference program's by a relative error of at most 0.0003.
Values may be sent and summed in bfloat16 or wider, within the bound.
No kernel may reach another device: no remote copies, remote signals or barrier semaphores. Data moves between devices by JAX's collectives and lax.ppermute only.
A program may use at most 128 MiB of HBM per device.

```python
import jax
import jax.numpy as jnp
from jax import lax

S = 256
RB_DEV = 2304
M = 18432
NB = 72
N_PROW = 8


def draw_block_live(key, part):
    group = RB_DEV // S
    groups = NB // group
    key_bits = jax.random.fold_in(key, 11)
    key_pick = jax.random.fold_in(key, 12)
    coins = jax.random.randint(key_bits, (NB,), 0, 2)
    picked = jax.random.randint(key_pick, (groups,), 0, group)
    within = jnp.arange(NB, dtype=jnp.int32) % group
    forced = (within == jnp.repeat(picked, group)).astype(jnp.int32)
    return jnp.maximum(coins, forced).astype(jnp.int32)


def level_of(own_key, dims, pieces, smallest, top_value):
    def one(position, parts):
        steps = jax.random.uniform(jax.random.fold_in(jax.random.fold_in(own_key, 6), position), (parts,), jnp.float32, smallest / len(pieces), top_value / len(pieces))
        return jnp.repeat(jnp.exp(steps), dims[position] // parts).reshape((-1,) + (1,) * (len(dims) - position - 1))

    gain = one(*pieces[0])
    for cut in pieces[1:]:
        gain = gain * one(*cut)
    return gain


def normal_values(rng, dims, deviation, reach, pieces=(), kind=jnp.bfloat16):
    array = deviation * jax.random.normal(rng, dims, jnp.float32)
    if pieces:
        array = array * level_of(rng, dims, pieces, -0.22, 0.18)
    return jnp.clip(array, -reach, reach).astype(kind)


def setup_inputs(seed: int = 0) -> dict:
    key_list = jax.random.split(jax.random.key(seed), 5)
    inverse_trailing = normal_values(key_list[0], (M, M), 1.0, 6.0, ((0, 8), (1, 4)))
    panel = normal_values(key_list[1], (M, S), (M // 2) ** -0.5, 0.0625, ((0, 8),))
    supernode_inverse = normal_values(key_list[2], (S, S), 1.0, 6.0, (), jnp.float32)
    block_live = draw_block_live(jax.random.fold_in(key_list[4], 71), 0)
    return {"inverse_trailing": inverse_trailing, "panel": panel, "supernode_inverse": supernode_inverse, "block_live": block_live}


def reference(inverse_trailing, panel, supernode_inverse, block_live):
    live = jnp.repeat(block_live, S).astype(jnp.float32)
    masked_panel = (panel.astype(jnp.float32) * live[:, None]).astype(jnp.bfloat16)
    blocks = inverse_trailing.reshape(N_PROW, RB_DEV, M)

    def block_rows(rows):
        return jnp.dot(rows, masked_panel, preferred_element_type=jnp.float32)

    product = lax.map(block_rows, blocks).reshape(M, S)
    column_inverse = -product * live[:, None]
    contracted = jnp.dot(masked_panel.astype(jnp.float32).T, column_inverse, precision=lax.Precision.HIGHEST)
    diagonal_inverse = supernode_inverse - contracted
    return column_inverse, diagonal_inverse
```

```python
import functools

import jax
import jax.numpy as jnp
from jax import lax
from jax.experimental import pallas as pl
from jax.experimental.pallas import tpu as pltpu
from jax.sharding import PartitionSpec as P

AXES = ("prow", "pcol")
TAIL = 16
STEPS = 64.0
TOP = 32760.0
LN2 = 0.6931471805599453
F32 = jnp.float32


def vmem():
    return pl.BlockSpec(memory_space=pltpu.VMEM)


def smem():
    return pl.BlockSpec(memory_space=pltpu.SMEM)


def quantize(x):
    top = jnp.maximum(jnp.max(jnp.abs(x), axis=0, keepdims=True), 1e-30)
    step = jnp.ceil(jnp.log(top) * (STEPS / LN2))
    scale = jnp.exp(step * (-LN2 / STEPS)) * TOP
    return jnp.round(x * scale).astype(jnp.int32).astype(jnp.int16), step


def widen(q, step):
    return q.astype(jnp.int32).astype(F32) * (jnp.exp(step * (LN2 / STEPS)) * (1.0 / TOP))


def store_message(ref, blocks, size):
    steps = []
    for i, x in enumerate(blocks):
        q, step = quantize(x)
        ref[i * size : (i + 1) * size, :] = q
        steps.append(step)
    width = ref.shape[1]
    pad = jnp.zeros((TAIL - len(steps), width), F32)
    tail = jnp.concatenate(steps + [pad], axis=0)
    ref[len(blocks) * size :, :] = tail.astype(jnp.int32).astype(jnp.int16)


def message_blocks(ref, count, size):
    tail = ref[count * size :, :].astype(jnp.int32).astype(F32)
    return [widen(ref[i * size : (i + 1) * size, :], tail[i : i + 1, :]) for i in range(count)]


def pack_kernel(idx, keep, panel, *outs, size, parts):
    half = panel.shape[1] // 2
    i = 0
    for part, count in enumerate(parts):
        for j in range(count):
            start = pl.multiple_of(idx[i] * size, size)
            block = panel[pl.ds(start, size), :].astype(F32) * keep[i].astype(F32)
            block = block.astype(panel.dtype)
            for h in range(2):
                outs[h * len(parts) + part][j * size : (j + 1) * size, :] = block[:, h * half : (h + 1) * half]
            i += 1


def product_kernel(rows, valid, cols, a, own, other, panel, part, message, term, scales, *, n, size):
    i = pl.program_id(0)
    count = pl.num_programs(0)
    acc = None
    for side, source in ((0, own), (1, other)):
        for j in range(n):
            start = pl.multiple_of(cols[side * n + j] * size, size)
            piece = jnp.dot(
                a[:, pl.ds(start, size)], source[j * size : (j + 1) * size, :], preferred_element_type=F32
            )
            acc = piece if acc is None else acc + piece
    acc = acc * valid[i].astype(F32)
    part[...] = acc
    q, step = quantize(acc)
    message[pl.ds(pl.multiple_of(i * size, size), size), :] = q
    contract = (((0,), (0,)), ((), ()))
    high = acc.astype(jnp.bfloat16)
    low = (acc - high.astype(F32)).astype(jnp.bfloat16)
    local = panel[...]
    piece = lax.dot_general(local, high, contract, preferred_element_type=F32) + lax.dot_general(
        local, low, contract, preferred_element_type=F32
    )

    @pl.when(i == 0)
    def _():
        scales[...] = jnp.zeros_like(scales)
        term[...] = piece

    @pl.when(i != 0)
    def _():
        term[...] = term[...] + piece

    scales[pl.ds(i, 1), :] = step

    @pl.when(i == count - 1)
    def _():
        message[message.shape[0] - TAIL :, :] = scales[...].astype(jnp.int32).astype(jnp.int16)


def join_kernel(part, came, message, *, count, size):
    blocks = message_blocks(came, count, size)
    store_message(message, [part[i * size : (i + 1) * size, :] + blocks[i] for i in range(count)], size)


def meet_kernel(mine, came, message, *, count, size):
    a = message_blocks(mine, count, size)
    b = message_blocks(came, count, size)
    store_message(message, [x + y for x, y in zip(a, b)], size)


def spread_kernel(idx, valid, live, *refs, layout, size):
    out = refs[-1]
    width = out.shape[1] // 2
    for b in range(out.shape[0] // size):

        @pl.when(live[b] == 0)
        def _():
            out[b * size : (b + 1) * size, :] = jnp.zeros((size, out.shape[1]), F32)

    for ref, (half, first, count) in zip(refs, layout):
        tail = ref[count * size :, :].astype(jnp.int32).astype(F32)
        for i in range(count):

            @pl.when(valid[first + i] != 0)
            def _():
                start = pl.multiple_of(idx[first + i] * size, size)
                value = widen(ref[i * size : (i + 1) * size, :], tail[i : i + 1, :])
                out[pl.ds(start, size), half * width : (half + 1) * width] = -value


def packed_order(live, n):
    b = live.shape[1]
    rank_live = jnp.cumsum(live, axis=1) - 1
    rank_dead = jnp.cumsum(1 - live, axis=1) - 1 + jnp.sum(live, axis=1, keepdims=True)
    rank = jnp.where(live != 0, rank_live, rank_dead)
    hit = (rank[:, None, :] == jnp.arange(n)[None, :, None]).astype(jnp.int32)
    order = jnp.sum(hit * jnp.arange(b)[None, None, :], axis=2)
    valid = jnp.sum(hit * live[:, None, :], axis=2)
    return order.astype(jnp.int32), valid.astype(jnp.int32)


def chunk_sizes(n):
    return {9: (2, 3, 4), 8: (2, 3, 3), 7: (2, 2, 3), 6: (2, 2, 2), 5: (1, 2, 2)}.get(n, (n,))


def body(inverse_trailing, panel, supernode_inverse, live, *, n, n_prow, n_pcol):
    rows_dev, width = panel.shape
    col_count = inverse_trailing.shape[1]
    groups, per = live.shape
    size = rows_dev // per
    half = width // 2
    ratio = n_prow // n_pcol
    prow = lax.axis_index("prow")
    pcol = lax.axis_index("pcol")
    order, valid = packed_order(live, n)
    pick = functools.partial(lax.dynamic_index_in_dim, keepdims=False)
    my_rows, my_valid, my_live = pick(order, prow), pick(valid, prow), pick(live, prow)
    core = prow % ratio
    own_group = pcol * ratio + core
    other_group = pcol * ratio + (ratio - 1 - core)
    cols = jnp.concatenate(
        [pick(order, own_group) + core * per, pick(order, other_group) + (ratio - 1 - core) * per]
    )

    def send(value, target):
        pairs = []
        for p in range(n_prow):
            for c in range(n_pcol):
                to = target(p, c)
                if to is not None:
                    pairs.append((p * n_pcol + c, to[0] * n_pcol + to[1]))
        return lax.ppermute(value, AXES, pairs)

    def place(p, c):
        return (p // ratio) ^ c

    is_root = (prow // ratio == pcol).astype(jnp.int32)
    parts = (n - n // 2, n // 2)
    packed = pl.pallas_call(
        functools.partial(pack_kernel, size=size, parts=parts),
        out_shape=[jax.ShapeDtypeStruct((count * size, half), panel.dtype) for _ in range(2) for count in parts],
        in_specs=[smem(), smem(), vmem()],
        out_specs=[vmem()] * 4,
    )(my_rows, my_valid * is_root, panel)
    swap = lambda p, c: (p ^ 1, c)
    halves = []
    for h in range(2):
        a, b = packed[2 * h : 2 * h + 2]
        if n_prow // ratio == 4:
            near_a = send(a, lambda p, c: (p ^ 2, c) if place(p, c) == 0 else None)
            near_b = send(b, lambda p, c: (p ^ 4, c) if place(p, c) == 0 else None)
            a = a + near_a
            b = b + near_b
            far_b = send(b, lambda p, c: (p ^ 2, c) if place(p, c) in (0, 2) else None)
            far_a = send(a, lambda p, c: (p ^ 4, c) if place(p, c) in (0, 1) else None)
            full = jnp.concatenate([a + far_a, b + far_b], axis=0)
        else:
            full = jnp.concatenate([a, b], axis=0)
            bit = 1
            while bit < n_prow // ratio:
                full = full + send(
                    full, lambda p, c, bit=bit: (p ^ (bit * ratio), c) if place(p, c) < bit else None
                )
                bit *= 2
        halves.append((full, send(full, swap)))

    chunks = chunk_sizes(n)
    middle = n_pcol // 2
    in_middle = jnp.logical_or(pcol == middle - 1, pcol == middle)
    terms, layout, results = [], [], []
    for h in range(2):
        first = 0
        for count in chunks if h == 0 else chunks[::-1]:
            msg_rows = count * size + TAIL
            part, message, term = pl.pallas_call(
                functools.partial(product_kernel, n=n, size=size),
                grid_spec=pltpu.PrefetchScalarGridSpec(
                    num_scalar_prefetch=3,
                    grid=(count,),
                    in_specs=[
                        pl.BlockSpec((size, col_count), lambda i, r, v, c: (r[i], 0)),
                        pl.BlockSpec((n * size, half), lambda i, r, v, c: (0, 0)),
                        pl.BlockSpec((n * size, half), lambda i, r, v, c: (0, 0)),
                        pl.BlockSpec((size, width), lambda i, r, v, c: (r[i], 0)),
                    ],
                    out_specs=[
                        pl.BlockSpec((size, half), lambda i, r, v, c: (i, 0)),
                        pl.BlockSpec((msg_rows, half), lambda i, r, v, c: (0, 0)),
                        pl.BlockSpec((width, half), lambda i, r, v, c: (0, 0)),
                    ],
                    scratch_shapes=[pltpu.VMEM((TAIL, half), F32)],
                ),
                out_shape=[
                    jax.ShapeDtypeStruct((count * size, half), F32),
                    jax.ShapeDtypeStruct((msg_rows, half), jnp.int16),
                    jax.ShapeDtypeStruct((width, half), F32),
                ],
            )(my_rows[first : first + count], my_valid[first : first + count], cols, inverse_trailing, *halves[h], panel)
            terms.append((h, term))
            results.append(sum_over_line(part, message, count, size, send, middle, n_pcol, in_middle))
            layout.append((h, first, count))
            first += count

    d = [sum(t for k, t in terms if k == h) for h in range(2)]
    d = jnp.concatenate(d, axis=1)
    step = 1
    while step < n_prow:
        d = d + send(d, lambda p, c, step=step: (p ^ step, c))
        step *= 2
    count = width // size * 2
    d = jnp.concatenate([d[:, :half], d[:, half:]], axis=0)
    message = pl.pallas_call(
        lambda x, o: store_message(o, [x[i * size : (i + 1) * size, :] for i in range(count)], size),
        out_shape=jax.ShapeDtypeStruct((2 * width + TAIL, half), jnp.int16),
        in_specs=[vmem()],
        out_specs=vmem(),
    )(d)
    diag_message = sum_over_line(d, message, count, size, send, middle, n_pcol, in_middle)

    def diagonal_kernel(base, ref, out):
        blocks = message_blocks(ref, count, size)
        per_half = count // 2
        for h in range(2):
            for i in range(per_half):
                s = slice(i * size, (i + 1) * size), slice(h * half, (h + 1) * half)
                out[s] = base[s] + blocks[h * per_half + i]

    diagonal_inverse = pl.pallas_call(
        diagonal_kernel,
        out_shape=jax.ShapeDtypeStruct((width, width), F32),
        in_specs=[vmem()] * 2,
        out_specs=vmem(),
    )(supernode_inverse, diag_message)
    column_inverse = pl.pallas_call(
        functools.partial(spread_kernel, layout=layout, size=size),
        out_shape=jax.ShapeDtypeStruct((rows_dev, width), F32),
        in_specs=[smem()] * 3 + [vmem()] * len(results),
        out_specs=vmem(),
    )(my_rows, my_valid, my_live, *results)
    return column_inverse, diagonal_inverse


def sum_over_line(part, message, count, size, send, middle, n_pcol, in_middle):
    shape = jax.ShapeDtypeStruct(message.shape, jnp.int16)
    for hop in range(middle - 1):
        def inwards(p, c, hop=hop):
            if c == hop:
                return p, c + 1
            if c == n_pcol - 1 - hop:
                return p, c - 1
            return None

        came = send(message, inwards)
        message = pl.pallas_call(
            functools.partial(join_kernel, count=count, size=size),
            out_shape=shape,
            in_specs=[vmem()] * 2,
            out_specs=vmem(),
        )(part, came)
    across = send(
        message, lambda p, c: (p, n_pcol - 1 - c) if c in (middle - 1, middle) else None
    )
    total = pl.pallas_call(
        functools.partial(meet_kernel, count=count, size=size),
        out_shape=shape,
        in_specs=[vmem()] * 2,
        out_specs=vmem(),
    )(message, across)
    total = jnp.where(in_middle, total, 0)
    for hop in range(middle - 1):
        def outwards(p, c, hop=hop):
            if c == middle - 1 - hop:
                return p, c - 1
            if c == middle + hop:
                return p, c + 1
            return None

        total = total + send(total, outwards)
    return total


def solution(mesh):
    n_prow, n_pcol = mesh.shape["prow"], mesh.shape["pcol"]

    def per_device(inverse_trailing, panel, supernode_inverse, block_live):
        per = block_live.shape[0] // n_prow
        live = block_live.reshape(n_prow, per)
        return body(inverse_trailing, panel, supernode_inverse, live, n=per, n_prow=n_prow, n_pcol=n_pcol)

    in_specs = (P("prow", "pcol"), P("prow", None), P(), P())
    out_specs = (P("prow", None), P())
    return jax.shard_map(
        per_device, mesh=mesh, in_specs=in_specs, out_specs=out_specs, check_vma=False
    )
```

```python
import functools

import jax
import jax.numpy as jnp
from jax import lax
from jax.experimental import pallas as pl
from jax.experimental.pallas import tpu as pltpu
from jax.sharding import PartitionSpec as P


AXES = ("prow", "pcol")
SMALLEST = 9
SCRATCH = 8 << 20
TAIL = 16
STEPS = 64.0
TOP = 32760.0
LN2 = 0.6931471805599453
F32 = jnp.float32
VMEM = pl.BlockSpec(memory_space=pltpu.VMEM)
SMEM = pl.BlockSpec(memory_space=pltpu.SMEM)
HBM = pl.BlockSpec(memory_space=pltpu.HBM)


def near(x):
    return pltpu.with_memory_space_constraint(x, pltpu.VMEM)


def kernel(body, outs, specs, out_specs, **options):
    params = pltpu.CompilerParams(vmem_limit_bytes=SCRATCH)
    return pl.pallas_call(
        body, out_shape=outs, in_specs=specs, out_specs=out_specs, compiler_params=params, **options
    )


def quantize(x):
    top = jnp.maximum(jnp.max(jnp.abs(x), axis=0, keepdims=True), 1e-30)
    step = jnp.ceil(jnp.log(top) * (STEPS / LN2))
    scale = jnp.exp(step * (-LN2 / STEPS)) * TOP
    return jnp.round(x * scale).astype(jnp.int32).astype(jnp.int16), step


def widen(q, step):
    return q.astype(jnp.int32).astype(F32) * (jnp.exp(step * (LN2 / STEPS)) * (1.0 / TOP))


def store_message(ref, blocks, size):
    steps = []
    for i, x in enumerate(blocks):
        q, step = quantize(x)
        ref[i * size : (i + 1) * size, :] = q
        steps.append(step)
    pad = jnp.zeros((TAIL - len(steps), ref.shape[1]), F32)
    tail = jnp.concatenate(steps + [pad], axis=0)
    ref[len(blocks) * size :, :] = tail.astype(jnp.int32).astype(jnp.int16)


def message_blocks(ref, size):
    count = (ref.shape[0] - TAIL) // size
    tail = ref[count * size :, :].astype(jnp.int32).astype(F32)
    return [widen(ref[i * size : (i + 1) * size, :], tail[i : i + 1, :]) for i in range(count)]


def is_middle(n_pcol):
    pcol = lax.axis_index("pcol")
    return jnp.logical_or(pcol == n_pcol // 2 - 1, pcol == n_pcol // 2)


def pack_kernel(live, panel, a, b, rows, cols, valid, *, n, per, ratio):
    size = panel.shape[0] // per
    split = a.shape[0] // size
    prow, pcol = lax.axis_index("prow"), lax.axis_index("pcol")
    core = prow % ratio
    a[...] = jnp.zeros_like(a)
    b[...] = jnp.zeros_like(b)
    for i in range(n):
        rows[i] = 0
        valid[i] = 0
        cols[i] = 0
        cols[n + i] = 0
    slot = 0
    for k in range(per):
        alive = live[prow * per + k] != 0

        @pl.when(alive)
        def _():
            rows[slot] = k
            valid[slot] = 1

        @pl.when(jnp.logical_and(alive, slot < split))
        def _():
            a[pl.ds(pl.multiple_of(slot * size, size), size), :] = panel[k * size : (k + 1) * size, :]

        @pl.when(jnp.logical_and(alive, slot >= split))
        def _():
            start = pl.multiple_of((slot - split) * size, size)
            b[pl.ds(start, size), :] = panel[k * size : (k + 1) * size, :]

        slot = slot + alive.astype(jnp.int32)
    for side in range(ratio):
        which = core if side == 0 else ratio - 1 - core
        slot = 0
        for k in range(per):
            alive = live[(pcol * ratio + which) * per + k] != 0

            @pl.when(alive)
            def _():
                cols[side * n + slot] = which * per + k

            slot = slot + alive.astype(jnp.int32)


def fetch_kernel(rows, cols, a, out, sem, *, first, size):
    for i in range(out.shape[0] // size):
        r = pl.multiple_of(rows[first + i] * size, size)

        def copy(j, _, i=i, r=r):
            c = pl.multiple_of(cols[j] * size, size)
            to = out.at[pl.ds(i * size, size), pl.ds(pl.multiple_of(j * size, size), size)]
            pltpu.make_async_copy(a.at[pl.ds(r, size), pl.ds(c, size)], to, sem).start()
            return 0

        lax.fori_loop(0, out.shape[1] // size, copy, 0, unroll=True)
    whole = a.at[pl.ds(0, out.shape[0]), pl.ds(0, out.shape[1])]
    pltpu.make_async_copy(whole, out, sem).wait()


def merge_kernel(a, xa, ya, da, b, xb, yb, db, full, *, ratio):
    root = lax.axis_index("prow") // ratio == lax.axis_index("pcol")
    top = a.shape[0]
    full[:top, :] = jnp.where(root, a[...], xa[...] + ya[...] + da[...])
    full[top:, :] = jnp.where(root, b[...], xb[...] + yb[...] + db[...])


def product_kernel(left, own, other, a, b, *refs, first, size):
    part, message, term = refs[-3:]
    n_rows = own.shape[0]
    acc = jnp.dot(left[:, :n_rows], own[...], preferred_element_type=F32)
    acc = acc + jnp.dot(left[:, n_rows:], other[...], preferred_element_type=F32)
    part[...] = acc
    count = left.shape[0] // size
    store_message(message, [acc[i * size : (i + 1) * size, :] for i in range(count)], size)
    contract = (((0,), (0,)), ((), ()))
    high = acc.astype(jnp.bfloat16)
    low = (acc - high.astype(F32)).astype(jnp.bfloat16)
    total = refs[0][...] if len(refs) == 4 else None
    split = a.shape[0] // size
    for i in range(count):
        at = first + i
        local = a[at * size : (at + 1) * size, :] if at < split else b[(at - split) * size : (at - split + 1) * size, :]
        for x in (high, low):
            piece = lax.dot_general(local, x[i * size : (i + 1) * size, :], contract, preferred_element_type=F32)
            total = piece if total is None else total + piece
    term[...] = total


def join_kernel(part, came, message, *, size):
    blocks = message_blocks(came, size)
    store_message(message, [part[i * size : (i + 1) * size, :] + x for i, x in enumerate(blocks)], size)


def meet_kernel(mine, came, message, *, size):
    pairs = zip(message_blocks(mine, size), message_blocks(came, size))
    store_message(message, [x + y for x, y in pairs], size)


def spread_kernel(rows, valid, live, total, came, *refs, first, size, per, n_pcol, fill):
    out, blocks, zeros, sem = refs[-4:]
    middle = is_middle(n_pcol)
    count = blocks.shape[0] // size
    prow = lax.axis_index("prow")

    def zero(k):
        return pltpu.make_async_copy(zeros, out.at[pl.ds(k * size, size), :], sem.at[count + k])

    def copy(i):
        start = pl.multiple_of(rows[first + i] * size, size)
        return pltpu.make_async_copy(blocks.at[pl.ds(i * size, size), :], out.at[pl.ds(start, size), :], sem.at[i])

    if fill:
        zeros[...] = jnp.zeros_like(zeros)
        for k in range(per):
            pl.when(live[prow * per + k] == 0)(lambda k=k: zero(k).start())
    picked = jnp.where(middle, total[...], came[...])
    tail = picked[count * size :, :].astype(jnp.int32).astype(F32)
    for i in range(count):
        blocks[i * size : (i + 1) * size, :] = -widen(picked[i * size : (i + 1) * size, :], tail[i : i + 1, :])
        pl.when(valid[first + i] != 0)(lambda i=i: copy(i).start())
    for i in range(count):
        pl.when(valid[first + i] != 0)(lambda i=i: copy(i).wait())
    if fill:
        for k in range(per):
            pl.when(live[prow * per + k] == 0)(lambda k=k: zero(k).wait())


def pick_kernel(total, came, out, *, n_pcol):
    out[...] = jnp.where(is_middle(n_pcol), total[...], came[...])


def add_kernel(x, y, out):
    out[...] = x[...] + y[...]


def halves_kernel(term, keep, give, *, ratio):
    core = lax.axis_index("prow") % ratio
    half = keep.shape[1]
    left, right = term[:, :half], term[:, half:]
    keep[...] = jnp.where(core == 0, left, right)
    give[...] = jnp.where(core == 0, right, left)


def root_kernel(a, b, out, *, ratio):
    root = lax.axis_index("prow") // ratio == lax.axis_index("pcol")
    top = a.shape[0]
    out[:top, :] = jnp.where(root, a[...], jnp.zeros_like(a))
    out[top:, :] = jnp.where(root, b[...], jnp.zeros_like(b))


def diagonal_kernel(base, mine, other, out, *, ratio):
    core = lax.axis_index("prow") % ratio
    half = out.shape[1] // ratio
    size = out.shape[0]
    left = jnp.where(core == 0, mine[...], other[...])
    right = jnp.where(core == 0, other[...], mine[...])
    for h, m in ((0, left), (1, right)):
        value = widen(m[:size, :], m[size : size + 1, :].astype(jnp.int32).astype(F32))
        out[:, h * half : (h + 1) * half] = base[:, h * half : (h + 1) * half] + value


def chunk_sizes(n):
    return {9: (2, 3, 2, 2), 8: (2, 2, 2, 2), 7: (2, 2, 2, 1), 6: (2, 2, 1, 1), 5: (2, 2, 1)}.get(n, (n,))


def packed_step(inverse_trailing, panel, supernode_inverse, block_live, *, n, n_prow, n_pcol):
    rows_dev, width = panel.shape
    per = block_live.shape[0] // n_prow
    size = rows_dev // per
    ratio = n_prow // n_pcol
    chips = n_prow // ratio

    def send(value, target):
        pairs = []
        for p in range(n_prow):
            for c in range(n_pcol):
                to = target(p, c)
                if to is not None:
                    pairs.append((p * n_pcol + c, to[0] * n_pcol + to[1]))
        return near(lax.ppermute(value, AXES, pairs))

    def place(p, c):
        return (p // ratio) ^ c

    inverse_trailing = pltpu.with_memory_space_constraint(inverse_trailing, pltpu.HBM)

    split = n - n // 2
    tables = [jax.ShapeDtypeStruct((k,), jnp.int32) for k in (n, 2 * n, n)]
    sides = [pltpu.VMEM((k * size, width), panel.dtype) for k in (split, n - split)]
    a, b, rows, cols, valid = kernel(
        functools.partial(pack_kernel, n=n, per=per, ratio=ratio),
        sides + tables, [SMEM, VMEM], [VMEM] * 2 + [SMEM] * 3,
    )(block_live, panel)

    def to_x(p, c):
        return (p ^ ratio, c)

    def to_y(p, c):
        return (p ^ (2 * ratio), c)

    def only(step, *places):
        return lambda p, c: step(p, c) if place(p, c) in places else None

    chunks = chunk_sizes(n)
    lefts = []
    first = 0
    for count in chunks:
        lefts.append(
            kernel(
                functools.partial(fetch_kernel, first=first, size=size),
                pltpu.VMEM((count * size, 2 * n * size), inverse_trailing.dtype), [SMEM, SMEM, HBM], VMEM,
                scratch_shapes=[pltpu.SemaphoreType.DMA],
            )(rows, cols, inverse_trailing)
        )
        first += count
    if chips == 4:
        xa = send(a, only(to_x, 0))
        yb = send(b, only(to_y, 0))
        xb = send(b, only(to_x, 0))
        ya = send(a, only(to_y, 0))
        da = send(xa, only(to_y, 1))
        db = send(yb, only(to_x, 2))
        own = kernel(
            functools.partial(merge_kernel, ratio=ratio),
            pltpu.VMEM((n * size, width), panel.dtype), [VMEM] * 8, VMEM,
        )(a, xa, ya, da, b, xb, yb, db)
    else:
        shape = pltpu.VMEM((n * size, width), panel.dtype)
        own = kernel(functools.partial(root_kernel, ratio=ratio), shape, [VMEM] * 2, VMEM)(a, b)
        bit = 1
        while bit < chips:
            def spread(p, c, bit=bit):
                return (p ^ (bit * ratio), c) if place(p, c) < bit else None

            own = kernel(add_kernel, shape, [VMEM] * 2, VMEM)(own, send(own, spread))
            bit *= 2
    swap = lambda p, c: (p ^ 1, c)
    other = send(own, swap)

    middle = n_pcol // 2

    def sum_over_line(part, message):
        out = pltpu.VMEM(message.shape, jnp.int16)
        for hop in range(middle - 1):
            def inwards(p, c, hop=hop):
                return {hop: (p, c + 1), n_pcol - 1 - hop: (p, c - 1)}.get(c)

            came = send(message, inwards)
            message = kernel(functools.partial(join_kernel, size=part_size), out, [VMEM] * 2, VMEM)(part, came)
        across = send(message, lambda p, c: (p, n_pcol - 1 - c) if c in (middle - 1, middle) else None)
        total = kernel(functools.partial(meet_kernel, size=part_size), out, [VMEM] * 2, VMEM)(message, across)
        came, value = None, total
        for hop in range(middle - 1):
            def outwards(p, c, hop=hop):
                return {middle - 1 - hop: (p, c - 1), middle + hop: (p, c + 1)}.get(c)

            value = send(value, outwards)
            came = value if came is None else kernel(add_kernel, out, [VMEM] * 2, VMEM)(came, value)
        return total, came

    part_size = size
    term, sums = None, []
    first = 0
    for k, count in enumerate(chunks):
        message_shape = (count * size + TAIL, width)
        part, message, term = kernel(
            functools.partial(product_kernel, first=first, size=size),
            [pltpu.VMEM((count * size, width), F32), pltpu.VMEM(message_shape, jnp.int16),
             pltpu.VMEM((width, width), F32)],
            [VMEM] * (5 if term is None else 6), [VMEM] * 3,
        )(lefts[k], own, other, a, b, *(() if term is None else (term,)))
        sums.append((first, count, *sum_over_line(part, message)))
        first += count

    half = width // ratio
    shape = pltpu.VMEM((width, half), F32)
    d, give = kernel(functools.partial(halves_kernel, ratio=ratio), [shape] * 2, [VMEM], [VMEM] * 2)(term)
    came = send(give, swap)
    step = ratio
    while True:
        d = kernel(add_kernel, shape, [VMEM] * 2, VMEM)(d, came)
        if step >= n_prow:
            break
        came = send(d, lambda p, c, step=step: (p ^ step, c))
        step *= 2
    part_size = width
    message = kernel(
        lambda x, o: store_message(o, [x[...]], width), pltpu.VMEM((width + TAIL, half), jnp.int16), [VMEM], VMEM
    )(d)
    total, came = sum_over_line(d, message)
    mine = kernel(
        functools.partial(pick_kernel, n_pcol=n_pcol), pltpu.VMEM(message.shape, jnp.int16), [VMEM] * 2, VMEM
    )(total, came)
    back = send(mine, swap)
    diagonal_inverse = kernel(
        functools.partial(diagonal_kernel, ratio=ratio), jax.ShapeDtypeStruct((width, width), F32), [VMEM] * 3, VMEM
    )(supernode_inverse, mine, back)

    result = None
    for first, count, total, came in sums:
        result = kernel(
            functools.partial(
                spread_kernel, first=first, size=size, per=per, n_pcol=n_pcol, fill=result is None
            ),
            jax.ShapeDtypeStruct((rows_dev, width), F32),
            [SMEM] * 3 + [VMEM] * 2 + ([] if result is None else [HBM]), HBM,
            scratch_shapes=[
                pltpu.VMEM((count * size, width), F32), pltpu.VMEM((size, width), F32),
                pltpu.SemaphoreType.DMA((count + per,)),
            ],
            input_output_aliases={} if result is None else {5: 0},
        )(rows, valid, block_live, total, came, *(() if result is None else (result,)))
    return result, diagonal_inverse


def solution(mesh):
    n_prow, n_pcol = mesh.shape["prow"], mesh.shape["pcol"]

    def per_device(inverse_trailing, panel, supernode_inverse, block_live):
        per = block_live.shape[0] // n_prow
        smallest = min(per, SMALLEST)

        def program(n):
            def run(*args):
                return packed_step(*args, n=n, n_prow=n_prow, n_pcol=n_pcol)

            return run

        programs = [program(n) for n in range(smallest, per + 1)]
        args = (inverse_trailing, panel, supernode_inverse, block_live)
        if len(programs) == 1:
            return programs[0](*args)
        counts = jnp.sum((block_live != 0).astype(jnp.int32).reshape(n_prow, per), axis=1)
        return lax.switch(jnp.max(counts) - smallest, programs, *args)

    in_specs = (P("prow", "pcol"), P("prow", None), P(), P())
    out_specs = (P("prow", None), P())
    return jax.shard_map(
        per_device, mesh=mesh, in_specs=in_specs, out_specs=out_specs, check_vma=False
    )
```

```python
import functools

import jax
import jax.numpy as jnp
from jax import lax
from jax.experimental import pallas as pl
from jax.experimental.pallas import tpu as pltpu
from jax.sharding import PartitionSpec as P


AXES = ("prow", "pcol")
SMALLEST = 9
SCRATCH = 8 << 20
ROWS = 64
TAIL = 16
STEPS = 64.0
TOP = 32760.0
LN2 = 0.6931471805599453
F32 = jnp.float32
VMEM = pl.BlockSpec(memory_space=pltpu.VMEM)
SMEM = pl.BlockSpec(memory_space=pltpu.SMEM)
HBM = pl.BlockSpec(memory_space=pltpu.HBM)


def near(x):
    return pltpu.with_memory_space_constraint(x, pltpu.VMEM)


def kernel(body, outs, specs, out_specs, **options):
    params = pltpu.CompilerParams(vmem_limit_bytes=SCRATCH)
    return pl.pallas_call(
        body, out_shape=outs, in_specs=specs, out_specs=out_specs, compiler_params=params, **options
    )


def step_of(top):
    return jnp.ceil(jnp.log(jnp.maximum(top, 1e-30)) * (STEPS / LN2))


def top_of(step):
    return jnp.exp(step * (LN2 / STEPS))


def to_ints(x, step):
    return jnp.round(x * (jnp.exp(step * (-LN2 / STEPS)) * TOP)).astype(jnp.int32).astype(jnp.int16)


def to_floats(q, step):
    return q.astype(jnp.int32).astype(F32) * (top_of(step) * (1.0 / TOP))


def read_steps(message):
    return message[message.shape[0] - TAIL :, :].astype(jnp.int32).astype(F32)


def write_steps(message, steps):
    message[message.shape[0] - TAIL :, :] = steps.astype(jnp.int32).astype(jnp.int16)


def by_rows(size, work):
    def one(r, _):
        work(r)
        return 0

    lax.fori_loop(0, size // ROWS, one, 0)


def rows_at(block, r, size):
    return pl.ds(pl.multiple_of(block * size + r * ROWS, ROWS), ROWS)


def store_message(message, part, size):
    count = part.shape[0] // size
    steps = []
    for i in range(count):
        top = jnp.max(jnp.abs(part[i * size : (i + 1) * size, :]), axis=0, keepdims=True)
        steps.append(step_of(top))

        def one(r, i=i):
            at = rows_at(i, r, size)
            message[at, :] = to_ints(part[at, :], steps[i])

        by_rows(size, one)
    pad = jnp.zeros((TAIL - count, message.shape[1]), F32)
    write_steps(message, jnp.concatenate(steps + [pad], axis=0))


def is_middle(n_pcol):
    pcol = lax.axis_index("pcol")
    return jnp.logical_or(pcol == n_pcol // 2 - 1, pcol == n_pcol // 2)


def pack_kernel(live, panel, *refs, ranges, n, per, ratio):
    packs, (rows, cols, valid, sem) = refs[:-4], refs[-4:]
    size = panel.shape[0] // per
    prow, pcol = lax.axis_index("prow"), lax.axis_index("pcol")
    core = prow % ratio

    def each_copy(act):
        slot = 0
        for k in range(per):
            alive = live[prow * per + k] != 0
            for (first, last), pack in zip(ranges, packs):
                inside = jnp.logical_and(slot >= first, slot < last)

                @pl.when(jnp.logical_and(alive, inside))
                def _():
                    start = pl.multiple_of((slot - first) * size, size)
                    act(
                        pltpu.make_async_copy(
                            panel.at[pl.ds(k * size, size), :], pack.at[pl.ds(start, size), :], sem
                        )
                    )

            slot = slot + alive.astype(jnp.int32)
        return slot

    count = each_copy(lambda copy: copy.start())
    for i in range(n):
        rows[i] = 0
        valid[i] = (count > i).astype(jnp.int32)
        cols[i] = 0
        cols[n + i] = 0
        for (first, last), pack in zip(ranges, packs):
            if first <= i < last:

                @pl.when(count <= i)
                def _():
                    at = slice((i - first) * size, (i - first + 1) * size)
                    pack[at, :] = jnp.zeros((size, pack.shape[1]), pack.dtype)

    slot = 0
    for k in range(per):
        alive = live[prow * per + k] != 0

        @pl.when(alive)
        def _():
            rows[slot] = k

        slot = slot + alive.astype(jnp.int32)
    for side in range(ratio):
        which = core if side == 0 else ratio - 1 - core
        slot = 0
        for k in range(per):
            alive = live[(pcol * ratio + which) * per + k] != 0

            @pl.when(alive)
            def _():
                cols[side * n + slot] = which * per + k

            slot = slot + alive.astype(jnp.int32)
    each_copy(lambda copy: copy.wait())


def fetch_kernel(rows, cols, a, out, sem, *, first, size):
    for i in range(out.shape[0] // size):
        r = pl.multiple_of(rows[first + i] * size, size)

        def copy(j, _, i=i, r=r):
            c = pl.multiple_of(cols[j] * size, size)
            to = out.at[pl.ds(i * size, size), pl.ds(pl.multiple_of(j * size, size), size)]
            pltpu.make_async_copy(a.at[pl.ds(r, size), pl.ds(c, size)], to, sem).start()
            return 0

        lax.fori_loop(0, out.shape[1] // size, copy, 0)
    whole = a.at[pl.ds(0, out.shape[0]), pl.ds(0, out.shape[1])]
    pltpu.make_async_copy(whole, out, sem).wait()


def merge_kernel(a, b, xa1, xa2, da1, da2, ya, yb1, yb2, db1, db2, xb, full, *, ratio):
    root = lax.axis_index("prow") // ratio == lax.axis_index("pcol")

    @pl.when(root)
    def _():
        full[: a.shape[0], :] = a[...]
        full[a.shape[0] :, :] = b[...]

    @pl.when(jnp.logical_not(root))
    def _():
        start = 0
        for whole, early, late in ((ya, (xa1, xa2), (da1, da2)), (xb, (yb1, yb2), (db1, db2))):
            inner = 0
            for e, l in zip(early, late):
                size = e.shape[0]
                full[start : start + size, :] = whole[inner : inner + size, :] + e[...] + l[...]
                start += size
                inner += size


def product_kernel(left, own, other, a, b, *refs, first, size):
    part, message, term = refs[-3:]
    n_rows = own.shape[0]
    acc = jnp.dot(left[:, :n_rows], own[...], preferred_element_type=F32)
    part[...] = acc + jnp.dot(left[:, n_rows:], other[...], preferred_element_type=F32)
    store_message(message, part, size)
    contract = (((0,), (0,)), ((), ()))
    total = refs[0][...] if len(refs) == 4 else None
    split = a.shape[0] // size
    for i in range(left.shape[0] // size):
        at = first + i
        local = a[at * size : (at + 1) * size, :] if at < split else b[(at - split) * size : (at - split + 1) * size, :]
        x = part[i * size : (i + 1) * size, :]
        high = x.astype(jnp.bfloat16)
        low = (x - high.astype(F32)).astype(jnp.bfloat16)
        for y in (high, low):
            piece = lax.dot_general(local, y, contract, preferred_element_type=F32)
            total = piece if total is None else total + piece
    term[...] = total


def join_kernel(part, mine, came, message, *, size):
    before, arrived = read_steps(mine), read_steps(came)
    steps = step_of(top_of(before) + top_of(arrived))
    write_steps(message, steps)
    for i in range(part.shape[0] // size):

        def one(r, i=i):
            at = rows_at(i, r, size)
            message[at, :] = to_ints(part[at, :] + to_floats(came[at, :], arrived[i : i + 1, :]), steps[i : i + 1, :])

        by_rows(size, one)


def meet_kernel(mine, came, message, *, size, n_pcol):
    low_side = lax.axis_index("pcol") < n_pcol // 2
    a, b = read_steps(mine), read_steps(came)
    steps = step_of(top_of(a) + top_of(b))
    write_steps(message, steps)
    first, second = jnp.where(low_side, a, b), jnp.where(low_side, b, a)
    for i in range((mine.shape[0] - TAIL) // size):

        def one(r, i=i):
            at = rows_at(i, r, size)
            x, y = mine[at, :], came[at, :]
            u, v = jnp.where(low_side, x, y), jnp.where(low_side, y, x)
            total = to_floats(u, first[i : i + 1, :]) + to_floats(v, second[i : i + 1, :])
            message[at, :] = to_ints(total, steps[i : i + 1, :])

        by_rows(size, one)


def spread_kernel(rows, valid, live, total, came, *refs, first, size, per, n_pcol, fill):
    out, blocks, zeros, sem = refs[-4:]
    middle = is_middle(n_pcol)
    count = blocks.shape[0] // size
    prow = lax.axis_index("prow")

    def zero(k):
        return pltpu.make_async_copy(zeros, out.at[pl.ds(k * size, size), :], sem.at[count + k])

    def copy(i):
        start = pl.multiple_of(rows[first + i] * size, size)
        return pltpu.make_async_copy(blocks.at[pl.ds(i * size, size), :], out.at[pl.ds(start, size), :], sem.at[i])

    if fill:
        zeros[...] = jnp.zeros_like(zeros)
        for k in range(per):
            pl.when(live[prow * per + k] == 0)(lambda k=k: zero(k).start())
    steps = jnp.where(middle, read_steps(total), read_steps(came))
    for i in range(count):

        def one(r, i=i):
            at = rows_at(i, r, size)
            blocks[at, :] = -to_floats(jnp.where(middle, total[at, :], came[at, :]), steps[i : i + 1, :])

        by_rows(size, one)
        pl.when(valid[first + i] != 0)(lambda i=i: copy(i).start())
    for i in range(count):
        pl.when(valid[first + i] != 0)(lambda i=i: copy(i).wait())
    if fill:
        for k in range(per):
            pl.when(live[prow * per + k] == 0)(lambda k=k: zero(k).wait())


def pick_kernel(total, came, out, *, n_pcol):
    out[...] = jnp.where(is_middle(n_pcol), total[...], came[...])


def add_kernel(x, y, out):
    out[...] = x[...] + y[...]


def halves_kernel(term, keep, give, *, ratio):
    core = lax.axis_index("prow") % ratio
    half = keep.shape[1]
    left, right = term[:, :half], term[:, half:]
    keep[...] = jnp.where(core == 0, left, right)
    give[...] = jnp.where(core == 0, right, left)


def root_kernel(a, b, out, *, ratio):
    root = lax.axis_index("prow") // ratio == lax.axis_index("pcol")
    top = a.shape[0]
    out[:top, :] = jnp.where(root, a[...], jnp.zeros_like(a))
    out[top:, :] = jnp.where(root, b[...], jnp.zeros_like(b))


def diagonal_kernel(base, mine, other, out, *, ratio):
    core = lax.axis_index("prow") % ratio
    half = out.shape[1] // ratio
    size = out.shape[0]
    left = jnp.where(core == 0, mine[...], other[...])
    right = jnp.where(core == 0, other[...], mine[...])
    for h, m in ((0, left), (1, right)):
        value = to_floats(m[:size, :], m[size : size + 1, :].astype(jnp.int32).astype(F32))
        out[:, h * half : (h + 1) * half] = base[:, h * half : (h + 1) * half] + value


def chunk_sizes(n):
    return {9: (3, 3, 2, 1), 8: (3, 2, 2, 1), 7: (3, 2, 1, 1), 6: (2, 2, 1, 1), 5: (2, 2, 1)}.get(n, (n,))


def packed_step(inverse_trailing, panel, supernode_inverse, block_live, *, n, n_prow, n_pcol):
    rows_dev, width = panel.shape
    per = block_live.shape[0] // n_prow
    size = rows_dev // per
    ratio = n_prow // n_pcol
    chips = n_prow // ratio

    def send(value, target):
        pairs = []
        for p in range(n_prow):
            for c in range(n_pcol):
                to = target(p, c)
                if to is not None:
                    pairs.append((p * n_pcol + c, to[0] * n_pcol + to[1]))
        return near(lax.ppermute(value, AXES, pairs))

    def place(p, c):
        return (p // ratio) ^ c

    inverse_trailing = pltpu.with_memory_space_constraint(inverse_trailing, pltpu.HBM)

    panel = pltpu.with_memory_space_constraint(panel, pltpu.HBM)

    split = n - n // 2
    cuts = (0, split - split // 2, split, n - (n - split) // 2, n)
    ranges = [(0, split), (split, n)] + list(zip(cuts[:-1], cuts[1:]))
    tables = [jax.ShapeDtypeStruct((k,), jnp.int32) for k in (n, 2 * n, n)]
    a, b, a1, a2, b1, b2, rows, cols, valid = kernel(
        functools.partial(pack_kernel, ranges=ranges, n=n, per=per, ratio=ratio),
        [pltpu.VMEM(((q - p) * size, width), panel.dtype) for p, q in ranges] + tables,
        [SMEM, HBM], [VMEM] * len(ranges) + [SMEM] * 3,
        scratch_shapes=[pltpu.SemaphoreType.DMA],
    )(block_live, panel)

    def to_x(p, c):
        return (p ^ ratio, c)

    def to_y(p, c):
        return (p ^ (2 * ratio), c)

    def only(step, *places):
        return lambda p, c: step(p, c) if place(p, c) in places else None

    chunks = chunk_sizes(n)
    lefts = []
    first = 0
    for count in chunks:
        lefts.append(
            kernel(
                functools.partial(fetch_kernel, first=first, size=size),
                pltpu.VMEM((count * size, 2 * n * size), inverse_trailing.dtype), [SMEM, SMEM, HBM], VMEM,
                scratch_shapes=[pltpu.SemaphoreType.DMA],
            )(rows, cols, inverse_trailing)
        )
        first += count
    if chips == 4:
        xa1 = send(a1, only(to_x, 0))
        yb1 = send(b1, only(to_y, 0))
        xa2 = send(a2, only(to_x, 0))
        yb2 = send(b2, only(to_y, 0))
        xb = send(b, only(to_x, 0))
        ya = send(a, only(to_y, 0))
        da1 = send(xa1, only(to_y, 1))
        db1 = send(yb1, only(to_x, 2))
        da2 = send(xa2, only(to_y, 1))
        db2 = send(yb2, only(to_x, 2))
        own = kernel(
            functools.partial(merge_kernel, ratio=ratio),
            pltpu.VMEM((n * size, width), panel.dtype), [VMEM] * 12, VMEM,
        )(a, b, xa1, xa2, da1, da2, ya, yb1, yb2, db1, db2, xb)
    else:
        shape = pltpu.VMEM((n * size, width), panel.dtype)
        own = kernel(functools.partial(root_kernel, ratio=ratio), shape, [VMEM] * 2, VMEM)(a, b)
        bit = 1
        while bit < chips:
            def spread(p, c, bit=bit):
                return (p ^ (bit * ratio), c) if place(p, c) < bit else None

            own = kernel(add_kernel, shape, [VMEM] * 2, VMEM)(own, send(own, spread))
            bit *= 2
    swap = lambda p, c: (p ^ 1, c)
    other = send(own, swap)

    middle = n_pcol // 2

    def sum_over_line(part, message):
        out = pltpu.VMEM(message.shape, jnp.int16)
        mine = message
        for hop in range(middle - 1):
            def inwards(p, c, hop=hop):
                return {hop: (p, c + 1), n_pcol - 1 - hop: (p, c - 1)}.get(c)

            came = send(message, inwards)
            message = kernel(functools.partial(join_kernel, size=part_size), out, [VMEM] * 3, VMEM)(part, mine, came)
        across = send(message, lambda p, c: (p, n_pcol - 1 - c) if c in (middle - 1, middle) else None)
        total = kernel(functools.partial(meet_kernel, size=part_size, n_pcol=n_pcol), out, [VMEM] * 2, VMEM)(message, across)
        came, value = None, total
        for hop in range(middle - 1):
            def outwards(p, c, hop=hop):
                return {middle - 1 - hop: (p, c - 1), middle + hop: (p, c + 1)}.get(c)

            value = send(value, outwards)
            came = value if came is None else kernel(add_kernel, out, [VMEM] * 2, VMEM)(came, value)
        return total, came

    part_size = size
    term, sums = None, []
    first = 0
    for k, count in enumerate(chunks):
        message_shape = (count * size + TAIL, width)
        part, message, term = kernel(
            functools.partial(product_kernel, first=first, size=size),
            [pltpu.VMEM((count * size, width), F32), pltpu.VMEM(message_shape, jnp.int16),
             pltpu.VMEM((width, width), F32)],
            [VMEM] * (5 if term is None else 6), [VMEM] * 3,
        )(lefts[k], own, other, a, b, *(() if term is None else (term,)))
        sums.append((first, count, *sum_over_line(part, message)))
        first += count

    half = width // ratio
    shape = pltpu.VMEM((width, half), F32)
    d, give = kernel(functools.partial(halves_kernel, ratio=ratio), [shape] * 2, [VMEM], [VMEM] * 2)(term)
    came = send(give, swap)
    step = ratio
    while True:
        d = kernel(add_kernel, shape, [VMEM] * 2, VMEM)(d, came)
        if step >= n_prow:
            break
        came = send(d, lambda p, c, step=step: (p ^ step, c))
        step *= 2
    part_size = width
    message = kernel(
        lambda x, o: store_message(o, x, width), pltpu.VMEM((width + TAIL, half), jnp.int16), [VMEM], VMEM
    )(d)
    total, came = sum_over_line(d, message)
    mine = kernel(
        functools.partial(pick_kernel, n_pcol=n_pcol), pltpu.VMEM(message.shape, jnp.int16), [VMEM] * 2, VMEM
    )(total, came)
    back = send(mine, swap)
    diagonal_inverse = kernel(
        functools.partial(diagonal_kernel, ratio=ratio), jax.ShapeDtypeStruct((width, width), F32), [VMEM] * 3, VMEM
    )(supernode_inverse, mine, back)

    result = None
    for first, count, total, came in sums:
      result = kernel(
          functools.partial(
              spread_kernel, first=first, size=size, per=per, n_pcol=n_pcol, fill=result is None
          ),
          jax.ShapeDtypeStruct((rows_dev, width), F32),
          [SMEM] * 3 + [VMEM] * 2 + ([] if result is None else [HBM]), HBM,
          scratch_shapes=[
              pltpu.VMEM((count * size, width), F32), pltpu.VMEM((size, width), F32),
              pltpu.SemaphoreType.DMA((count + per,)),
          ],
          input_output_aliases={} if result is None else {5: 0},
      )(rows, valid, block_live, total, came, *(() if result is None else (result,)))
    return result, diagonal_inverse


def solution(mesh):
    n_prow, n_pcol = mesh.shape["prow"], mesh.shape["pcol"]

    def per_device(inverse_trailing, panel, supernode_inverse, block_live):
        per = block_live.shape[0] // n_prow
        smallest = min(per, SMALLEST)

        def program(n):
            def run(*args):
                return packed_step(*args, n=n, n_prow=n_prow, n_pcol=n_pcol)

            return run

        programs = [program(n) for n in range(smallest, per + 1)]
        args = (inverse_trailing, panel, supernode_inverse, block_live)
        if len(programs) == 1:
            return programs[0](*args)
        counts = jnp.sum((block_live != 0).astype(jnp.int32).reshape(n_prow, per), axis=1)
        return lax.switch(jnp.max(counts) - smallest, programs, *args)

    in_specs = (P("prow", "pcol"), P("prow", None), P(), P())
    out_specs = (P("prow", None), P())
    return jax.shard_map(
        per_device, mesh=mesh, in_specs=in_specs, out_specs=out_specs, check_vma=False
    )
```

```python
import functools

import jax
import jax.numpy as jnp
from jax import lax
from jax.experimental import pallas as pl
from jax.experimental.pallas import tpu as pltpu
from jax.sharding import PartitionSpec as P


AXES = ("prow", "pcol")
SMALLEST = 7
SCRATCH = 8 << 20
ROWS = 64
TAIL = 16
STEPS = 64.0
TOP = 32760.0
LN2 = 0.6931471805599453
F32 = jnp.float32
VMEM = pl.BlockSpec(memory_space=pltpu.VMEM)
SMEM = pl.BlockSpec(memory_space=pltpu.SMEM)
HBM = pl.BlockSpec(memory_space=pltpu.HBM)


def near(x):
    return pltpu.with_memory_space_constraint(x, pltpu.VMEM)


def kernel(body, outs, specs, out_specs, **options):
    params = pltpu.CompilerParams(vmem_limit_bytes=SCRATCH)
    return pl.pallas_call(
        body, out_shape=outs, in_specs=specs, out_specs=out_specs, compiler_params=params, **options
    )


def step_of(top):
    return jnp.ceil(jnp.log(jnp.maximum(top, 1e-30)) * (STEPS / LN2))


def top_of(step):
    return jnp.exp(step * (LN2 / STEPS))


def to_ints(x, step):
    return jnp.round(x * (jnp.exp(step * (-LN2 / STEPS)) * TOP)).astype(jnp.int32).astype(jnp.int16)


def to_floats(q, step):
    return q.astype(jnp.int32).astype(F32) * (top_of(step) * (1.0 / TOP))


def read_steps(message):
    return message[message.shape[0] - TAIL :, :].astype(jnp.int32).astype(F32)


def write_steps(message, steps):
    message[message.shape[0] - TAIL :, :] = steps.astype(jnp.int32).astype(jnp.int16)


def by_rows(size, work):
    def one(r, _):
        work(r)
        return 0

    lax.fori_loop(0, size // ROWS, one, 0)


def rows_from(start, r):
    return pl.ds(pl.multiple_of(start + r * ROWS, ROWS), ROWS)


def rows_at(block, r, size):
    return pl.ds(pl.multiple_of(block * size + r * ROWS, ROWS), ROWS)


def store_message(message, part, size):
    count = part.shape[0] // size
    steps = []
    for i in range(count):
        top = jnp.max(jnp.abs(part[i * size : (i + 1) * size, :]), axis=0, keepdims=True)
        steps.append(step_of(top))

        def one(r, i=i):
            at = rows_at(i, r, size)
            message[at, :] = to_ints(part[at, :], steps[i])

        by_rows(size, one)
    pad = jnp.zeros((TAIL - count, message.shape[1]), F32)
    write_steps(message, jnp.concatenate(steps + [pad], axis=0))


def is_middle(n_pcol):
    pcol = lax.axis_index("pcol")
    return jnp.logical_or(pcol == n_pcol // 2 - 1, pcol == n_pcol // 2)


def pack_kernel(live, panel, *refs, ranges, n, per, ratio):
    packs, (rows, cols, valid, sem) = refs[:-4], refs[-4:]
    size = panel.shape[0] // per
    prow, pcol = lax.axis_index("prow"), lax.axis_index("pcol")
    core = prow % ratio

    def each_copy(act):
        slot = 0
        for k in range(per):
            alive = live[prow * per + k] != 0
            for (first, last), pack in zip(ranges, packs):
                inside = jnp.logical_and(slot >= first, slot < last)

                @pl.when(jnp.logical_and(alive, inside))
                def _():
                    start = pl.multiple_of((slot - first) * size, size)
                    act(
                        pltpu.make_async_copy(
                            panel.at[pl.ds(k * size, size), :], pack.at[pl.ds(start, size), :], sem
                        )
                    )

            slot = slot + alive.astype(jnp.int32)
        return slot

    count = each_copy(lambda copy: copy.start())
    for i in range(n):
        rows[i] = 0
        valid[i] = (count > i).astype(jnp.int32)
        cols[i] = 0
        cols[n + i] = 0
        for (first, last), pack in zip(ranges, packs):
            if first <= i < last:

                @pl.when(count <= i)
                def _():
                    at = slice((i - first) * size, (i - first + 1) * size)
                    pack[at, :] = jnp.zeros((size, pack.shape[1]), pack.dtype)

    slot = 0
    for k in range(per):
        alive = live[prow * per + k] != 0

        @pl.when(alive)
        def _():
            rows[slot] = k

        slot = slot + alive.astype(jnp.int32)
    for side in range(ratio):
        which = core if side == 0 else ratio - 1 - core
        slot = 0
        for k in range(per):
            alive = live[(pcol * ratio + which) * per + k] != 0

            @pl.when(alive)
            def _():
                cols[side * n + slot] = which * per + k

            slot = slot + alive.astype(jnp.int32)
    each_copy(lambda copy: copy.wait())


def fetch_kernel(rows, cols, a, out, sem, *, first, size):
    for i in range(out.shape[0] // size):
        r = pl.multiple_of(rows[first + i] * size, size)

        def copy(j, _, i=i, r=r):
            c = pl.multiple_of(cols[j] * size, size)
            to = out.at[pl.ds(i * size, size), pl.ds(pl.multiple_of(j * size, size), size)]
            pltpu.make_async_copy(a.at[pl.ds(r, size), pl.ds(c, size)], to, sem).start()
            return 0

        lax.fori_loop(0, out.shape[1] // size, copy, 0)
    whole = a.at[pl.ds(0, out.shape[0]), pl.ds(0, out.shape[1])]
    pltpu.make_async_copy(whole, out, sem).wait()


def merge_kernel(a, b, xa1, xa2, da1, da2, ya, yb1, yb2, db1, db2, xb, full, *, ratio):
    root = lax.axis_index("prow") // ratio == lax.axis_index("pcol")

    @pl.when(root)
    def _():
        for source, to in ((a, 0), (b, a.shape[0])):

            def one(r, source=source, to=to):
                full[rows_from(to, r), :] = source[rows_from(0, r), :]

            by_rows(source.shape[0], one)

    @pl.when(jnp.logical_not(root))
    def _():
        start = 0
        for whole, early, late in ((ya, (xa1, xa2), (da1, da2)), (xb, (yb1, yb2), (db1, db2))):
            inner = 0
            for e, l in zip(early, late):

                def one(r, whole=whole, e=e, l=l, start=start, inner=inner):
                    at = rows_from(0, r)
                    full[rows_from(start, r), :] = whole[rows_from(inner, r), :] + e[at, :] + l[at, :]

                by_rows(e.shape[0], one)
                start += e.shape[0]
                inner += e.shape[0]


def product_kernel(left, own, other, a, b, *refs, first, size):
    part, message, term = refs[-3:]
    n_rows = own.shape[0]

    def one(i, _):
        at = pl.ds(pl.multiple_of(i * size, size), size)
        acc = jnp.dot(left[at, :n_rows], own[...], preferred_element_type=F32)
        part[at, :] = acc + jnp.dot(left[at, n_rows:], other[...], preferred_element_type=F32)
        return 0

    lax.fori_loop(0, left.shape[0] // size, one, 0)
    store_message(message, part, size)
    contract = (((0,), (0,)), ((), ()))
    total = refs[0][...] if len(refs) == 4 else None
    split = a.shape[0] // size
    for i in range(left.shape[0] // size):
        at = first + i
        local = a[at * size : (at + 1) * size, :] if at < split else b[(at - split) * size : (at - split + 1) * size, :]
        x = part[i * size : (i + 1) * size, :]
        high = x.astype(jnp.bfloat16)
        low = (x - high.astype(F32)).astype(jnp.bfloat16)
        for y in (high, low):
            piece = lax.dot_general(local, y, contract, preferred_element_type=F32)
            total = piece if total is None else total + piece
    term[...] = total


def join_kernel(part, mine, came, message, *, size):
    before, arrived = read_steps(mine), read_steps(came)
    steps = step_of(top_of(before) + top_of(arrived))
    write_steps(message, steps)
    for i in range(part.shape[0] // size):

        def one(r, i=i):
            at = rows_at(i, r, size)
            message[at, :] = to_ints(part[at, :] + to_floats(came[at, :], arrived[i : i + 1, :]), steps[i : i + 1, :])

        by_rows(size, one)


def meet_kernel(mine, came, message, *, size, n_pcol):
    low_side = lax.axis_index("pcol") < n_pcol // 2
    a, b = read_steps(mine), read_steps(came)
    steps = step_of(top_of(a) + top_of(b))
    write_steps(message, steps)
    first, second = jnp.where(low_side, a, b), jnp.where(low_side, b, a)
    for i in range((mine.shape[0] - TAIL) // size):

        def one(r, i=i):
            at = rows_at(i, r, size)
            x, y = mine[at, :], came[at, :]
            u, v = jnp.where(low_side, x, y), jnp.where(low_side, y, x)
            total = to_floats(u, first[i : i + 1, :]) + to_floats(v, second[i : i + 1, :])
            message[at, :] = to_ints(total, steps[i : i + 1, :])

        by_rows(size, one)


def spread_kernel(rows, valid, live, total, came, *refs, first, size, per, n_pcol, fill):
    out, blocks, zeros, sem = refs[-4:]
    middle = is_middle(n_pcol)
    count = blocks.shape[0] // size
    prow = lax.axis_index("prow")

    def zero(k):
        return pltpu.make_async_copy(zeros, out.at[pl.ds(k * size, size), :], sem.at[count + k])

    def copy(i):
        start = pl.multiple_of(rows[first + i] * size, size)
        return pltpu.make_async_copy(blocks.at[pl.ds(i * size, size), :], out.at[pl.ds(start, size), :], sem.at[i])

    if fill:
        zeros[...] = jnp.zeros_like(zeros)
        for k in range(per):
            pl.when(live[prow * per + k] == 0)(lambda k=k: zero(k).start())
    steps = jnp.where(middle, read_steps(total), read_steps(came))
    for i in range(count):

        def one(r, i=i):
            at = rows_at(i, r, size)
            blocks[at, :] = -to_floats(jnp.where(middle, total[at, :], came[at, :]), steps[i : i + 1, :])

        by_rows(size, one)
        pl.when(valid[first + i] != 0)(lambda i=i: copy(i).start())
    for i in range(count):
        pl.when(valid[first + i] != 0)(lambda i=i: copy(i).wait())
    if fill:
        for k in range(per):
            pl.when(live[prow * per + k] == 0)(lambda k=k: zero(k).wait())


def pick_kernel(total, came, out, *, n_pcol):
    out[...] = jnp.where(is_middle(n_pcol), total[...], came[...])


def capacity_kernel(live, out, *, groups, per):
    most = 0
    for g in range(groups):
        count = 0
        for k in range(per):
            count = count + (live[g * per + k] != 0).astype(jnp.int32)
        most = jnp.maximum(most, count)
    out[0] = most


def add_kernel(x, y, out):
    out[...] = x[...] + y[...]


def halves_kernel(term, keep, give, *, ratio):
    core = lax.axis_index("prow") % ratio
    half = keep.shape[1]
    left, right = term[:, :half], term[:, half:]
    keep[...] = jnp.where(core == 0, left, right)
    give[...] = jnp.where(core == 0, right, left)


def root_kernel(a, b, out, *, ratio):
    root = lax.axis_index("prow") // ratio == lax.axis_index("pcol")
    top = a.shape[0]
    out[:top, :] = jnp.where(root, a[...], jnp.zeros_like(a))
    out[top:, :] = jnp.where(root, b[...], jnp.zeros_like(b))


def diagonal_kernel(base, mine, other, out, *, ratio):
    core = lax.axis_index("prow") % ratio
    half = out.shape[1] // ratio
    size = out.shape[0]
    left = jnp.where(core == 0, mine[...], other[...])
    right = jnp.where(core == 0, other[...], mine[...])
    for h, m in ((0, left), (1, right)):
        value = to_floats(m[:size, :], m[size : size + 1, :].astype(jnp.int32).astype(F32))
        out[:, h * half : (h + 1) * half] = base[:, h * half : (h + 1) * half] + value


def chunk_sizes(n):
    return {9: (3, 2, 2, 2), 8: (2, 2, 2, 2), 7: (2, 2, 2, 1)}.get(n, (n,))


def packed_step(inverse_trailing, panel, supernode_inverse, block_live, *, n, n_prow, n_pcol):
    rows_dev, width = panel.shape
    per = block_live.shape[0] // n_prow
    size = rows_dev // per
    ratio = n_prow // n_pcol
    chips = n_prow // ratio

    def send(value, target):
        pairs = []
        for p in range(n_prow):
            for c in range(n_pcol):
                to = target(p, c)
                if to is not None:
                    pairs.append((p * n_pcol + c, to[0] * n_pcol + to[1]))
        return near(lax.ppermute(value, AXES, pairs))

    def place(p, c):
        return (p // ratio) ^ c

    inverse_trailing = pltpu.with_memory_space_constraint(inverse_trailing, pltpu.HBM)

    panel = pltpu.with_memory_space_constraint(panel, pltpu.HBM)

    split = n - n // 2
    cuts = (0, split - split // 2, split, n - (n - split) // 2, n)
    ranges = [(0, split), (split, n)] + list(zip(cuts[:-1], cuts[1:]))
    tables = [jax.ShapeDtypeStruct((k,), jnp.int32) for k in (n, 2 * n, n)]
    a, b, a1, a2, b1, b2, rows, cols, valid = kernel(
        functools.partial(pack_kernel, ranges=ranges, n=n, per=per, ratio=ratio),
        [pltpu.VMEM(((q - p) * size, width), panel.dtype) for p, q in ranges] + tables,
        [SMEM, HBM], [VMEM] * len(ranges) + [SMEM] * 3,
        scratch_shapes=[pltpu.SemaphoreType.DMA],
    )(block_live, panel)

    def to_x(p, c):
        return (p ^ ratio, c)

    def to_y(p, c):
        return (p ^ (2 * ratio), c)

    def only(step, *places):
        return lambda p, c: step(p, c) if place(p, c) in places else None

    chunks = chunk_sizes(n)
    lefts = []
    first = 0
    for count in chunks:
        lefts.append(
            kernel(
                functools.partial(fetch_kernel, first=first, size=size),
                pltpu.VMEM((count * size, 2 * n * size), inverse_trailing.dtype), [SMEM, SMEM, HBM], VMEM,
                scratch_shapes=[pltpu.SemaphoreType.DMA],
            )(rows, cols, inverse_trailing)
        )
        first += count
    if chips == 4:
        xa1 = send(a1, only(to_x, 0))
        yb1 = send(b1, only(to_y, 0))
        xa2 = send(a2, only(to_x, 0))
        yb2 = send(b2, only(to_y, 0))
        xb = send(b, only(to_x, 0))
        ya = send(a, only(to_y, 0))
        da1 = send(xa1, only(to_y, 1))
        db1 = send(yb1, only(to_x, 2))
        da2 = send(xa2, only(to_y, 1))
        db2 = send(yb2, only(to_x, 2))
        own = kernel(
            functools.partial(merge_kernel, ratio=ratio),
            pltpu.VMEM((n * size, width), panel.dtype), [VMEM] * 12, VMEM,
        )(a, b, xa1, xa2, da1, da2, ya, yb1, yb2, db1, db2, xb)
    else:
        shape = pltpu.VMEM((n * size, width), panel.dtype)
        own = kernel(functools.partial(root_kernel, ratio=ratio), shape, [VMEM] * 2, VMEM)(a, b)
        bit = 1
        while bit < chips:
            def spread(p, c, bit=bit):
                return (p ^ (bit * ratio), c) if place(p, c) < bit else None

            own = kernel(add_kernel, shape, [VMEM] * 2, VMEM)(own, send(own, spread))
            bit *= 2
    swap = lambda p, c: (p ^ 1, c)
    other = send(own, swap)

    middle = n_pcol // 2

    def sum_over_line(part, message):
        out = pltpu.VMEM(message.shape, jnp.int16)
        mine = message
        for hop in range(middle - 1):
            def inwards(p, c, hop=hop):
                return {hop: (p, c + 1), n_pcol - 1 - hop: (p, c - 1)}.get(c)

            came = send(message, inwards)
            message = kernel(functools.partial(join_kernel, size=part_size), out, [VMEM] * 3, VMEM)(part, mine, came)
        across = send(message, lambda p, c: (p, n_pcol - 1 - c) if c in (middle - 1, middle) else None)
        total = kernel(functools.partial(meet_kernel, size=part_size, n_pcol=n_pcol), out, [VMEM] * 2, VMEM)(message, across)
        came, value = None, total
        for hop in range(middle - 1):
            def outwards(p, c, hop=hop):
                return {middle - 1 - hop: (p, c - 1), middle + hop: (p, c + 1)}.get(c)

            value = send(value, outwards)
            came = value if came is None else kernel(add_kernel, out, [VMEM] * 2, VMEM)(came, value)
        return total, came

    part_size = size
    term, sums = None, []
    first = 0
    for k, count in enumerate(chunks):
        message_shape = (count * size + TAIL, width)
        part, message, term = kernel(
            functools.partial(product_kernel, first=first, size=size),
            [pltpu.VMEM((count * size, width), F32), pltpu.VMEM(message_shape, jnp.int16),
             pltpu.VMEM((width, width), F32)],
            [VMEM] * (5 if term is None else 6), [VMEM] * 3,
        )(lefts[k], own, other, a, b, *(() if term is None else (term,)))
        sums.append((first, count, *sum_over_line(part, message)))
        first += count

    half = width // ratio
    shape = pltpu.VMEM((width, half), F32)
    d, give = kernel(functools.partial(halves_kernel, ratio=ratio), [shape] * 2, [VMEM], [VMEM] * 2)(term)
    came = send(give, swap)
    step = ratio
    while True:
        d = kernel(add_kernel, shape, [VMEM] * 2, VMEM)(d, came)
        if step >= n_prow:
            break
        came = send(d, lambda p, c, step=step: (p ^ step, c))
        step *= 2
    part_size = width
    message = kernel(
        lambda x, o: store_message(o, x, width), pltpu.VMEM((width + TAIL, half), jnp.int16), [VMEM], VMEM
    )(d)
    total, came = sum_over_line(d, message)
    mine = kernel(
        functools.partial(pick_kernel, n_pcol=n_pcol), pltpu.VMEM(message.shape, jnp.int16), [VMEM] * 2, VMEM
    )(total, came)
    back = send(mine, swap)
    diagonal_inverse = kernel(
        functools.partial(diagonal_kernel, ratio=ratio), jax.ShapeDtypeStruct((width, width), F32), [VMEM] * 3, VMEM
    )(supernode_inverse, mine, back)

    result = None
    for first, count, total, came in sums:
      result = kernel(
          functools.partial(
              spread_kernel, first=first, size=size, per=per, n_pcol=n_pcol, fill=result is None
          ),
          jax.ShapeDtypeStruct((rows_dev, width), F32),
          [SMEM] * 3 + [VMEM] * 2 + ([] if result is None else [HBM]), HBM,
          scratch_shapes=[
              pltpu.VMEM((count * size, width), F32), pltpu.VMEM((size, width), F32),
              pltpu.SemaphoreType.DMA((count + per,)),
          ],
          input_output_aliases={} if result is None else {5: 0},
      )(rows, valid, block_live, total, came, *(() if result is None else (result,)))
    return result, diagonal_inverse


def solution(mesh):
    n_prow, n_pcol = mesh.shape["prow"], mesh.shape["pcol"]

    def per_device(inverse_trailing, panel, supernode_inverse, block_live):
        per = block_live.shape[0] // n_prow
        smallest = min(per, SMALLEST)

        def program(n):
            def run(*args):
                return packed_step(*args, n=n, n_prow=n_prow, n_pcol=n_pcol)

            return run

        programs = [program(n) for n in range(smallest, per + 1)]
        args = (inverse_trailing, panel, supernode_inverse, block_live)
        if len(programs) == 1:
            return programs[0](*args)
        most = kernel(
            functools.partial(capacity_kernel, groups=n_prow, per=per),
            jax.ShapeDtypeStruct((1,), jnp.int32), [SMEM], SMEM,
        )(block_live)
        return lax.switch(most[0] - smallest, programs, *args)

    in_specs = (P("prow", "pcol"), P("prow", None), P(), P())
    out_specs = (P("prow", None), P())
    return jax.shard_map(
        per_device, mesh=mesh, in_specs=in_specs, out_specs=out_specs, check_vma=False
    )
```

```python
import functools

import jax
import jax.numpy as jnp
from jax import lax
from jax.experimental import pallas as pl
from jax.experimental.pallas import tpu as pltpu
from jax.sharding import PartitionSpec as P


AXES = ("prow", "pcol")
SMALLEST = 7
SCRATCH = 8 << 20
ROWS = 32
TAIL = 16
STEPS = 64.0
TOP = 32760.0
LN2 = 0.6931471805599453
F32 = jnp.float32
VMEM = pl.BlockSpec(memory_space=pltpu.VMEM)
SMEM = pl.BlockSpec(memory_space=pltpu.SMEM)
HBM = pl.BlockSpec(memory_space=pltpu.HBM)


def near(x):
    return pltpu.with_memory_space_constraint(x, pltpu.VMEM)


def kernel(body, outs, specs, out_specs, **options):
    params = pltpu.CompilerParams(vmem_limit_bytes=SCRATCH)
    return pl.pallas_call(
        body, out_shape=outs, in_specs=specs, out_specs=out_specs, compiler_params=params, **options
    )


def step_of(top):
    return jnp.ceil(jnp.log(jnp.maximum(top, 1e-30)) * (STEPS / LN2))


def top_of(step):
    return jnp.exp(step * (LN2 / STEPS))


def to_ints(x, step):
    return jnp.round(x * (jnp.exp(step * (-LN2 / STEPS)) * TOP)).astype(jnp.int32).astype(jnp.int16)


def to_floats(q, step):
    return q.astype(jnp.int32).astype(F32) * (top_of(step) * (1.0 / TOP))


def read_steps(message):
    return message[message.shape[0] - TAIL :, :].astype(jnp.int32).astype(F32)


def write_steps(message, steps):
    message[message.shape[0] - TAIL :, :] = steps.astype(jnp.int32).astype(jnp.int16)


def by_rows(size, work):
    def one(r, _):
        work(r)
        return 0

    lax.fori_loop(0, size // ROWS, one, 0)


def rows_from(start, r):
    return pl.ds(pl.multiple_of(start + r * ROWS, ROWS), ROWS)


def rows_at(block, r, size):
    return pl.ds(pl.multiple_of(block * size + r * ROWS, ROWS), ROWS)


def store_message(message, part, size):
    count = part.shape[0] // size
    steps = []
    for i in range(count):
        top = jnp.max(jnp.abs(part[i * size : (i + 1) * size, :]), axis=0, keepdims=True)
        steps.append(step_of(top))

        def one(r, i=i):
            at = rows_at(i, r, size)
            message[at, :] = to_ints(part[at, :], steps[i])

        by_rows(size, one)
    pad = jnp.zeros((TAIL - count, message.shape[1]), F32)
    write_steps(message, jnp.concatenate(steps + [pad], axis=0))


def is_middle(n_pcol):
    pcol = lax.axis_index("pcol")
    return jnp.logical_or(pcol == n_pcol // 2 - 1, pcol == n_pcol // 2)


def pack_kernel(live, panel, *refs, ranges, n, per, ratio):
    packs, (rows, cols, valid, sem) = refs[:-4], refs[-4:]
    size = panel.shape[0] // per
    prow, pcol = lax.axis_index("prow"), lax.axis_index("pcol")
    core = prow % ratio

    def each_copy(act):
        slot = 0
        for k in range(per):
            alive = live[prow * per + k] != 0
            for (first, last), pack in zip(ranges, packs):
                inside = jnp.logical_and(slot >= first, slot < last)

                @pl.when(jnp.logical_and(alive, inside))
                def _():
                    start = pl.multiple_of((slot - first) * size, size)
                    act(
                        pltpu.make_async_copy(
                            panel.at[pl.ds(k * size, size), :], pack.at[pl.ds(start, size), :], sem
                        )
                    )

            slot = slot + alive.astype(jnp.int32)
        return slot

    count = each_copy(lambda copy: copy.start())
    for i in range(n):
        rows[i] = 0
        valid[i] = (count > i).astype(jnp.int32)
        cols[i] = 0
        cols[n + i] = 0
        for (first, last), pack in zip(ranges, packs):
            if first <= i < last:

                @pl.when(count <= i)
                def _():
                    at = slice((i - first) * size, (i - first + 1) * size)
                    pack[at, :] = jnp.zeros((size, pack.shape[1]), pack.dtype)

    slot = 0
    for k in range(per):
        alive = live[prow * per + k] != 0

        @pl.when(alive)
        def _():
            rows[slot] = k

        slot = slot + alive.astype(jnp.int32)
    for side in range(ratio):
        which = core if side == 0 else ratio - 1 - core
        slot = 0
        for k in range(per):
            alive = live[(pcol * ratio + which) * per + k] != 0

            @pl.when(alive)
            def _():
                cols[side * n + slot] = which * per + k

            slot = slot + alive.astype(jnp.int32)
    each_copy(lambda copy: copy.wait())


def fetch_kernel(rows, cols, a, out, sem, *, first, size):
    for i in range(out.shape[0] // size):
        r = pl.multiple_of(rows[first + i] * size, size)

        def copy(j, _, i=i, r=r):
            c = pl.multiple_of(cols[j] * size, size)
            to = out.at[pl.ds(i * size, size), pl.ds(pl.multiple_of(j * size, size), size)]
            pltpu.make_async_copy(a.at[pl.ds(r, size), pl.ds(c, size)], to, sem).start()
            return 0

        lax.fori_loop(0, out.shape[1] // size, copy, 0)
    whole = a.at[pl.ds(0, out.shape[0]), pl.ds(0, out.shape[1])]
    pltpu.make_async_copy(whole, out, sem).wait()


def merge_kernel(a, b, xa1, xa2, da1, da2, ya, yb1, yb2, db1, db2, xb, full, *, ratio):
    root = lax.axis_index("prow") // ratio == lax.axis_index("pcol")

    @pl.when(root)
    def _():
        for source, to in ((a, 0), (b, a.shape[0])):

            def one(r, source=source, to=to):
                full[rows_from(to, r), :] = source[rows_from(0, r), :]

            by_rows(source.shape[0], one)

    @pl.when(jnp.logical_not(root))
    def _():
        start = 0
        for whole, early, late in ((ya, (xa1, xa2), (da1, da2)), (xb, (yb1, yb2), (db1, db2))):
            inner = 0
            for e, l in zip(early, late):

                def one(r, whole=whole, e=e, l=l, start=start, inner=inner):
                    at = rows_from(0, r)
                    full[rows_from(start, r), :] = whole[rows_from(inner, r), :] + e[at, :] + l[at, :]

                by_rows(e.shape[0], one)
                start += e.shape[0]
                inner += e.shape[0]


def early_kernel(left, own, part, *, size):
    def one(i, _):
        at = pl.ds(pl.multiple_of(i * size, size), size)
        part[at, :] = jnp.dot(left[at, : own.shape[0]], own[...], preferred_element_type=F32)
        return 0

    lax.fori_loop(0, left.shape[0] // size, one, 0)


def product_kernel(left, own, other, a, b, *refs, first, size):
    part, message, term = refs[-3:]
    n_rows = other.shape[0]

    def one(i, _):
        at = pl.ds(pl.multiple_of(i * size, size), size)
        if own.dtype == F32:
            acc = own[at, :]
        else:
            acc = jnp.dot(left[at, :n_rows], own[...], preferred_element_type=F32)
        part[at, :] = acc + jnp.dot(left[at, n_rows:], other[...], preferred_element_type=F32)
        return 0

    lax.fori_loop(0, left.shape[0] // size, one, 0)
    store_message(message, part, size)
    contract = (((0,), (0,)), ((), ()))
    total = refs[0][...] if len(refs) == 4 else None
    split = a.shape[0] // size
    for i in range(left.shape[0] // size):
        at = first + i
        local = a[at * size : (at + 1) * size, :] if at < split else b[(at - split) * size : (at - split + 1) * size, :]
        x = part[i * size : (i + 1) * size, :]
        high = x.astype(jnp.bfloat16)
        low = (x - high.astype(F32)).astype(jnp.bfloat16)
        for y in (high, low):
            piece = lax.dot_general(local, y, contract, preferred_element_type=F32)
            total = piece if total is None else total + piece
    term[...] = total


def join_kernel(part, mine, came, message, *, size):
    before, arrived = read_steps(mine), read_steps(came)
    steps = step_of(top_of(before) + top_of(arrived))
    write_steps(message, steps)
    for i in range(part.shape[0] // size):

        def one(r, i=i):
            at = rows_at(i, r, size)
            message[at, :] = to_ints(part[at, :] + to_floats(came[at, :], arrived[i : i + 1, :]), steps[i : i + 1, :])

        by_rows(size, one)


def meet_kernel(mine, came, message, *, size, n_pcol):
    low_side = lax.axis_index("pcol") < n_pcol // 2
    a, b = read_steps(mine), read_steps(came)
    steps = step_of(top_of(a) + top_of(b))
    write_steps(message, steps)
    first, second = jnp.where(low_side, a, b), jnp.where(low_side, b, a)
    for i in range((mine.shape[0] - TAIL) // size):

        def one(r, i=i):
            at = rows_at(i, r, size)
            x, y = mine[at, :], came[at, :]
            u, v = jnp.where(low_side, x, y), jnp.where(low_side, y, x)
            total = to_floats(u, first[i : i + 1, :]) + to_floats(v, second[i : i + 1, :])
            message[at, :] = to_ints(total, steps[i : i + 1, :])

        by_rows(size, one)


def spread_kernel(rows, valid, live, total, came, *refs, first, size, per, n_pcol, fill):
    out, blocks, zeros, sem = refs[-4:]
    middle = is_middle(n_pcol)
    count = blocks.shape[0] // size
    prow = lax.axis_index("prow")

    def zero(k):
        return pltpu.make_async_copy(zeros, out.at[pl.ds(k * size, size), :], sem.at[count + k])

    def copy(i):
        start = pl.multiple_of(rows[first + i] * size, size)
        return pltpu.make_async_copy(blocks.at[pl.ds(i * size, size), :], out.at[pl.ds(start, size), :], sem.at[i])

    if fill:
        zeros[...] = jnp.zeros_like(zeros)
        for k in range(per):
            pl.when(live[prow * per + k] == 0)(lambda k=k: zero(k).start())
    steps = jnp.where(middle, read_steps(total), read_steps(came))
    for i in range(count):

        def one(r, i=i):
            at = rows_at(i, r, size)
            blocks[at, :] = -to_floats(jnp.where(middle, total[at, :], came[at, :]), steps[i : i + 1, :])

        by_rows(size, one)
        pl.when(valid[first + i] != 0)(lambda i=i: copy(i).start())
    for i in range(count):
        pl.when(valid[first + i] != 0)(lambda i=i: copy(i).wait())
    if fill:
        for k in range(per):
            pl.when(live[prow * per + k] == 0)(lambda k=k: zero(k).wait())


def pick_kernel(total, came, out, *, n_pcol):
    out[...] = jnp.where(is_middle(n_pcol), total[...], came[...])


def capacity_kernel(live, out, *, groups, per):
    most = 0
    for g in range(groups):
        count = 0
        for k in range(per):
            count = count + (live[g * per + k] != 0).astype(jnp.int32)
        most = jnp.maximum(most, count)
    out[0] = most


def add_kernel(x, y, out):
    out[...] = x[...] + y[...]


def halves_kernel(term, keep, give, *, ratio):
    core = lax.axis_index("prow") % ratio
    half = keep.shape[1]
    left, right = term[:, :half], term[:, half:]
    keep[...] = jnp.where(core == 0, left, right)
    give[...] = jnp.where(core == 0, right, left)


def root_kernel(a, b, out, *, ratio):
    root = lax.axis_index("prow") // ratio == lax.axis_index("pcol")
    top = a.shape[0]
    out[:top, :] = jnp.where(root, a[...], jnp.zeros_like(a))
    out[top:, :] = jnp.where(root, b[...], jnp.zeros_like(b))


def diagonal_kernel(base, mine, other, out, *, ratio):
    core = lax.axis_index("prow") % ratio
    half = out.shape[1] // ratio
    size = out.shape[0]
    left = jnp.where(core == 0, mine[...], other[...])
    right = jnp.where(core == 0, other[...], mine[...])
    for h, m in ((0, left), (1, right)):
        value = to_floats(m[:size, :], m[size : size + 1, :].astype(jnp.int32).astype(F32))
        out[:, h * half : (h + 1) * half] = base[:, h * half : (h + 1) * half] + value


def chunk_sizes(n):
    return {9: (3, 2, 2, 2), 8: (2, 2, 2, 2), 7: (2, 2, 2, 1)}.get(n, (n,))


def packed_step(inverse_trailing, panel, supernode_inverse, block_live, *, n, n_prow, n_pcol):
    rows_dev, width = panel.shape
    per = block_live.shape[0] // n_prow
    size = rows_dev // per
    ratio = n_prow // n_pcol
    chips = n_prow // ratio

    def send(value, target):
        pairs = []
        for p in range(n_prow):
            for c in range(n_pcol):
                to = target(p, c)
                if to is not None:
                    pairs.append((p * n_pcol + c, to[0] * n_pcol + to[1]))
        return near(lax.ppermute(value, AXES, pairs))

    def place(p, c):
        return (p // ratio) ^ c

    inverse_trailing = pltpu.with_memory_space_constraint(inverse_trailing, pltpu.HBM)

    panel = pltpu.with_memory_space_constraint(panel, pltpu.HBM)

    split = n - n // 2
    cuts = (0, split - split // 2, split, n - (n - split) // 2, n)
    ranges = [(0, split), (split, n)] + list(zip(cuts[:-1], cuts[1:]))
    tables = [jax.ShapeDtypeStruct((k,), jnp.int32) for k in (n, 2 * n, n)]
    a, b, a1, a2, b1, b2, rows, cols, valid = kernel(
        functools.partial(pack_kernel, ranges=ranges, n=n, per=per, ratio=ratio),
        [pltpu.VMEM(((q - p) * size, width), panel.dtype) for p, q in ranges] + tables,
        [SMEM, HBM], [VMEM] * len(ranges) + [SMEM] * 3,
        scratch_shapes=[pltpu.SemaphoreType.DMA],
    )(block_live, panel)

    def to_x(p, c):
        return (p ^ ratio, c)

    def to_y(p, c):
        return (p ^ (2 * ratio), c)

    def only(step, *places):
        return lambda p, c: step(p, c) if place(p, c) in places else None

    chunks = chunk_sizes(n)
    lefts = []
    first = 0
    for count in chunks:
        lefts.append(
            kernel(
                functools.partial(fetch_kernel, first=first, size=size),
                pltpu.VMEM((count * size, 2 * n * size), inverse_trailing.dtype), [SMEM, SMEM, HBM], VMEM,
                scratch_shapes=[pltpu.SemaphoreType.DMA],
            )(rows, cols, inverse_trailing)
        )
        first += count
    if chips == 4:
        xa1 = send(a1, only(to_x, 0))
        yb1 = send(b1, only(to_y, 0))
        xa2 = send(a2, only(to_x, 0))
        yb2 = send(b2, only(to_y, 0))
        xb = send(b, only(to_x, 0))
        ya = send(a, only(to_y, 0))
        da1 = send(xa1, only(to_y, 1))
        db1 = send(yb1, only(to_x, 2))
        da2 = send(xa2, only(to_y, 1))
        db2 = send(yb2, only(to_x, 2))
        own = kernel(
            functools.partial(merge_kernel, ratio=ratio),
            pltpu.VMEM((n * size, width), panel.dtype), [VMEM] * 12, VMEM,
        )(a, b, xa1, xa2, da1, da2, ya, yb1, yb2, db1, db2, xb)
    else:
        shape = pltpu.VMEM((n * size, width), panel.dtype)
        own = kernel(functools.partial(root_kernel, ratio=ratio), shape, [VMEM] * 2, VMEM)(a, b)
        bit = 1
        while bit < chips:
            def spread(p, c, bit=bit):
                return (p ^ (bit * ratio), c) if place(p, c) < bit else None

            own = kernel(add_kernel, shape, [VMEM] * 2, VMEM)(own, send(own, spread))
            bit *= 2
    swap = lambda p, c: (p ^ 1, c)
    other = send(own, swap)
    early = kernel(
        functools.partial(early_kernel, size=size),
        pltpu.VMEM((chunks[0] * size, width), F32), [VMEM] * 2, VMEM,
    )(lefts[0], own)

    middle = n_pcol // 2

    def sum_over_line(part, message):
        out = pltpu.VMEM(message.shape, jnp.int16)
        mine = message
        for hop in range(middle - 1):
            def inwards(p, c, hop=hop):
                return {hop: (p, c + 1), n_pcol - 1 - hop: (p, c - 1)}.get(c)

            came = send(message, inwards)
            message = kernel(functools.partial(join_kernel, size=part_size), out, [VMEM] * 3, VMEM)(part, mine, came)
        across = send(message, lambda p, c: (p, n_pcol - 1 - c) if c in (middle - 1, middle) else None)
        total = kernel(functools.partial(meet_kernel, size=part_size, n_pcol=n_pcol), out, [VMEM] * 2, VMEM)(message, across)
        came, value = None, total
        for hop in range(middle - 1):
            def outwards(p, c, hop=hop):
                return {middle - 1 - hop: (p, c - 1), middle + hop: (p, c + 1)}.get(c)

            value = send(value, outwards)
            came = value if came is None else kernel(add_kernel, out, [VMEM] * 2, VMEM)(came, value)
        return total, came

    part_size = size
    term, sums = None, []
    first = 0
    for k, count in enumerate(chunks):
        message_shape = (count * size + TAIL, width)
        part, message, term = kernel(
            functools.partial(product_kernel, first=first, size=size),
            [pltpu.VMEM((count * size, width), F32), pltpu.VMEM(message_shape, jnp.int16),
             pltpu.VMEM((width, width), F32)],
            [VMEM] * (5 if term is None else 6), [VMEM] * 3,
        )(lefts[k], own if k else early, other, a, b, *(() if term is None else (term,)))
        sums.append((first, count, *sum_over_line(part, message)))
        first += count

    half = width // ratio
    shape = pltpu.VMEM((width, half), F32)
    d, give = kernel(functools.partial(halves_kernel, ratio=ratio), [shape] * 2, [VMEM], [VMEM] * 2)(term)
    came = send(give, swap)
    step = ratio
    while True:
        d = kernel(add_kernel, shape, [VMEM] * 2, VMEM)(d, came)
        if step >= n_prow:
            break
        came = send(d, lambda p, c, step=step: (p ^ step, c))
        step *= 2
    part_size = width
    message = kernel(
        lambda x, o: store_message(o, x, width), pltpu.VMEM((width + TAIL, half), jnp.int16), [VMEM], VMEM
    )(d)
    total, came = sum_over_line(d, message)
    mine = kernel(
        functools.partial(pick_kernel, n_pcol=n_pcol), pltpu.VMEM(message.shape, jnp.int16), [VMEM] * 2, VMEM
    )(total, came)
    back = send(mine, swap)
    diagonal_inverse = kernel(
        functools.partial(diagonal_kernel, ratio=ratio), jax.ShapeDtypeStruct((width, width), F32), [VMEM] * 3, VMEM
    )(supernode_inverse, mine, back)

    result = None
    for first, count, total, came in sums:
      result = kernel(
          functools.partial(
              spread_kernel, first=first, size=size, per=per, n_pcol=n_pcol, fill=result is None
          ),
          jax.ShapeDtypeStruct((rows_dev, width), F32),
          [SMEM] * 3 + [VMEM] * 2 + ([] if result is None else [HBM]), HBM,
          scratch_shapes=[
              pltpu.VMEM((count * size, width), F32), pltpu.VMEM((size, width), F32),
              pltpu.SemaphoreType.DMA((count + per,)),
          ],
          input_output_aliases={} if result is None else {5: 0},
      )(rows, valid, block_live, total, came, *(() if result is None else (result,)))
    return result, diagonal_inverse


def solution(mesh):
    n_prow, n_pcol = mesh.shape["prow"], mesh.shape["pcol"]

    def per_device(inverse_trailing, panel, supernode_inverse, block_live):
        per = block_live.shape[0] // n_prow
        smallest = min(per, SMALLEST)

        def program(n):
            def run(*args):
                return packed_step(*args, n=n, n_prow=n_prow, n_pcol=n_pcol)

            return run

        programs = [program(n) for n in range(smallest, per + 1)]
        args = (inverse_trailing, panel, supernode_inverse, block_live)
        if len(programs) == 1:
            return programs[0](*args)
        most = kernel(
            functools.partial(capacity_kernel, groups=n_prow, per=per),
            jax.ShapeDtypeStruct((1,), jnp.int32), [SMEM], SMEM,
        )(block_live)
        return lax.switch(most[0] - smallest, programs, *args)

    in_specs = (P("prow", "pcol"), P("prow", None), P(), P())
    out_specs = (P("prow", None), P())
    return jax.shard_map(
        per_device, mesh=mesh, in_specs=in_specs, out_specs=out_specs, check_vma=False
    )
```
